32 devices in a mesh: rep: 4 (over y, x), exp: 8 (over z, core).
Axes of the slice: x: 2, y: 2, z: 4, core: 2. Of those that a mesh axis runs over, the one named last changes fastest.
Arguments:
- tokens: bfloat16 [4096, 3584], P(('rep', 'exp')), may hold values from -6 to 6
- routes: int32 [4096, 8], P(('rep', 'exp')), may hold values from 0 to 255, as said below
- gates: float32 [4096, 8], P(('rep', 'exp')), may hold values from 0.1 to 1
- gate_weight: bfloat16 [8, 3584, 2048], P('exp', None, 'rep'), may hold values from -0.09375 to 0.09375
- up_weight: bfloat16 [8, 3584, 2048], P('exp', None, 'rep'), may hold values from -0.09375 to 0.09375
- down_weight: bfloat16 [8, 2048, 3584], P('exp', 'rep'), may hold values from -0.125 to 0.125
- grad_out: bfloat16 [4096, 3584], P(('rep', 'exp')), may hold values from -6 to 6
Outputs:
- combined: bfloat16 [4096, 3584], P(('rep', 'exp'))
- token_grad: bfloat16 [4096, 3584], P(('rep', 'exp'))
- gate_weight_grad: bfloat16 [8, 3584, 2048], P('exp', None, 'rep')
- up_weight_grad: bfloat16 [8, 3584, 2048], P('exp', None, 'rep')
- down_weight_grad: bfloat16 [8, 2048, 3584], P('exp', 'rep')
The draws below stay inside these ranges and needn't reach their ends.
Inputs may be any that keep to these rules, and one draw needn't show every extreme that they name: `routes`: each row names 8 different experts and at most one of experts 0 to 7. In the rows of one device (aligned blocks of 128 rows) each of experts 0 to 7 is named by at most 2 rows, and one of them, the same in every block, by exactly 2 rows.
All inputs are finite; a program needn't handle non-finite values.
Results may differ from the reference program's by a relative error of at most 0.012.
Values may be sent and summed in bfloat16 or wider, within the bound.
A program may use at most 128 MiB of HBM per device.

```python
import jax
import jax.numpy as jnp
from jax import lax

D = 3584
FF = 2048
EXPERTS = 256
TOP = 8
CAP = 2
TOK_DEV = 128
TOKENS = 4096
N_REP = 4
N_EXP = 8


def draw_routes(key, part):
    blocks = N_REP * N_EXP
    live_count = N_EXP
    spare_ids = EXPERTS - live_count
    stride = spare_ids // TOP
    slot_total = live_count * CAP
    key_hot, key_counts, key_perm, key_column, key_first = jax.random.split(key, 5)
    hottest = jax.random.randint(key_hot, (), 0, live_count)
    counts = jax.random.randint(key_counts, (blocks, live_count), 0, CAP + 1)
    counts = jnp.where(jnp.arange(live_count)[None, :] == hottest, CAP, counts)
    orders = jax.vmap(lambda sub_key: jax.random.permutation(sub_key, TOK_DEV))(jax.random.split(key_perm, blocks))
    slot_ids = jnp.arange(slot_total)
    slot_expert = slot_ids // CAP
    slot_rank = slot_ids % CAP
    is_live = slot_rank[None, :] < counts[:, slot_expert]
    targets = orders[:, :slot_total]
    inside = jnp.full((blocks, TOK_DEV), -1, jnp.int32)
    inside = inside.at[jnp.arange(blocks)[:, None], targets].set(jnp.where(is_live, slot_expert[None, :], -1).astype(jnp.int32))
    inside = inside.reshape(blocks * TOK_DEV)
    column = jax.random.randint(key_column, (blocks * TOK_DEV,), 0, TOP)
    first_id = jax.random.randint(key_first, (blocks * TOK_DEV,), 0, spare_ids)
    outside = live_count + (first_id[:, None] + jnp.arange(TOP)[None, :] * stride) % spare_ids
    chosen = (jnp.arange(TOP)[None, :] == column[:, None]) & (inside[:, None] >= 0)
    return jnp.where(chosen, inside[:, None], outside).astype(jnp.int32)


def levels(stream_key, extent, shards, least, high):
    gain, own = 1.0, jax.random.fold_in(stream_key, 6)
    for dim, parts in shards:
        draws = jnp.exp(jax.random.uniform(jax.random.fold_in(own, dim), (parts,), jnp.float32, least / len(shards), high / len(shards)))
        gain = gain * jnp.repeat(draws, extent[dim] // parts).reshape([-1 if axis == dim else 1 for axis in range(len(extent))])
    return gain


def normal_values(rng, extent, spread, most, cuts=(), held_as=jnp.bfloat16):
    values = spread * jax.random.normal(rng, extent, jnp.float32)
    if cuts:
        values = values * levels(rng, extent, cuts, -0.22, 0.18)
    return jnp.clip(values, -most, most).astype(held_as)


def setup_inputs(seed: int = 0) -> dict:
    keys = jax.random.split(jax.random.key(seed), 8)
    return {
        "tokens": normal_values(keys[0], (TOKENS, D), 1.0, 6.0, ((0, 32),)),
        "routes": draw_routes(jax.random.fold_in(keys[7], 71), 0),
        "gates": jnp.clip(0.1 + 0.9 * jax.random.uniform(keys[2], (TOKENS, TOP), jnp.float32) ** levels(keys[2], (TOKENS, TOP), ((0, 32),), -0.2, 0.2), 0.1, 1.0),
        "gate_weight": normal_values(keys[3], (N_EXP, D, FF), D ** -0.5, 0.09375, ((0, 8), (2, 4))),
        "up_weight": normal_values(keys[4], (N_EXP, D, FF), D ** -0.5, 0.09375, ((0, 8), (2, 4))),
        "down_weight": normal_values(keys[5], (N_EXP, FF, D), FF ** -0.5, 0.125, ((0, 8), (1, 4))),
        "grad_out": normal_values(keys[6], (TOKENS, D), 1.0, 6.0, ((0, 32),)),
    }


def block_sum(left, right, pattern):
    rounded = lax.optimization_barrier(jnp.einsum(pattern, left, right).astype(jnp.bfloat16))
    return jnp.sum(rounded.astype(jnp.float32), axis=1)


def reference(tokens, routes, gates, gate_weight, up_weight, down_weight, grad_out):
    capacity = N_REP * N_EXP * CAP
    blocks = N_REP
    block_units = FF // blocks
    live_count = N_EXP
    total_tokens = tokens.shape[0]
    features = tokens.shape[1]
    token_ids = jnp.arange(total_tokens, dtype=jnp.int32)

    def per_expert(carry, inputs):
        out_total, grad_total = carry
        expert, w_gate, w_up, w_down = inputs
        matches = routes == expert
        picked = jnp.any(matches, axis=1)
        weight = jnp.sum(jnp.where(matches, gates, jnp.zeros((), gates.dtype)), axis=1)
        order = (jnp.cumsum(picked.astype(jnp.int32)) - 1).astype(jnp.int32)
        target = jnp.where(picked, order, capacity).astype(jnp.int32)
        source = jnp.zeros((capacity + 1,), jnp.int32).at[target].set(token_ids)[:capacity]
        filled = jnp.zeros((capacity + 1,), gates.dtype).at[target].set(1.0)[:capacity]
        row_gate = weight[source] * filled
        rows_in = jnp.where(filled[:, None] > 0, tokens[source], jnp.zeros((), tokens.dtype))
        gate_pre = jnp.dot(rows_in, w_gate, preferred_element_type=jnp.float32)
        up_pre = jnp.dot(rows_in, w_up, preferred_element_type=jnp.float32)
        sigmoid_gate = jax.nn.sigmoid(gate_pre)
        active = gate_pre * sigmoid_gate
        hidden = (active * up_pre).astype(jnp.bfloat16)
        expert_out = block_sum(
            hidden.astype(jnp.float32).reshape(capacity, blocks, block_units),
            w_down.astype(jnp.float32).reshape(blocks, block_units, features),
            "rbf,bfd->rbd").astype(jnp.bfloat16)
        out_total = out_total.at[source].add(row_gate[:, None] * expert_out.astype(jnp.float32))
        out_grad = (row_gate[:, None] * grad_out[source].astype(jnp.float32)).astype(jnp.bfloat16)
        hidden_grad = jnp.dot(out_grad, w_down.T, preferred_element_type=jnp.float32)
        gate_grad = (hidden_grad * up_pre * sigmoid_gate * (1.0 + gate_pre * (1.0 - sigmoid_gate))).astype(jnp.bfloat16)
        up_grad = (hidden_grad * active).astype(jnp.bfloat16)
        down_grad = jnp.dot(hidden.T, out_grad, preferred_element_type=jnp.float32).astype(jnp.bfloat16)
        gate_wgrad = jnp.dot(rows_in.T, gate_grad, preferred_element_type=jnp.float32).astype(jnp.bfloat16)
        up_wgrad = jnp.dot(rows_in.T, up_grad, preferred_element_type=jnp.float32).astype(jnp.bfloat16)
        both_grad = jnp.concatenate([
            gate_grad.astype(jnp.float32).reshape(capacity, blocks, block_units),
            up_grad.astype(jnp.float32).reshape(capacity, blocks, block_units)], axis=2)
        both_weight = jnp.concatenate([
            w_gate.astype(jnp.float32).reshape(features, blocks, block_units),
            w_up.astype(jnp.float32).reshape(features, blocks, block_units)], axis=2)
        pair_grad = block_sum(both_grad, both_weight, "rbf,dbf->rbd").astype(jnp.bfloat16)
        grad_total = grad_total.at[source].add(pair_grad.astype(jnp.float32) * filled[:, None])
        return (out_total, grad_total), (gate_wgrad, up_wgrad, down_grad)

    start_total = jnp.zeros((total_tokens, features), jnp.float32)
    experts_iota = jnp.arange(live_count, dtype=jnp.int32)
    (out_total, grad_total), (gate_grads, up_grads, down_grads) = lax.scan(
        per_expert, (start_total, start_total), (experts_iota, gate_weight, up_weight, down_weight))
    combined = out_total.astype(jnp.bfloat16)
    token_grad = grad_total.astype(jnp.bfloat16)
    return (combined, token_grad, gate_grads, up_grads, down_grads)
```

```python
import functools

import jax
import jax.numpy as jnp
from jax import lax
from jax.experimental import pallas as pl
from jax.experimental.pallas import tpu as pltpu
from jax.sharding import PartitionSpec as P

CAP = 2
MESH = pl.DeviceIdType.MESH
F32 = jnp.float32
BF16 = jnp.bfloat16
LAST = (((1,), (1,)), ((), ()))
FIRST = (((0,), (0,)), ((), ()))


def exchange_kernel(
    R,
    E,
    routes,
    gates,
    tok_h,
    grad_h,
    wg_h,
    wu_h,
    wd_h,
    rows_o,
    hid_o,
    gg_o,
    ug_o,
    ret_o,
    place_o,
    w_o,
    tg_v,
    wg_v,
    wu_v,
    wd_v,
    sendb,
    land,
    xf,
    part,
    rs,
    back,
    ret,
    in_sem,
    own_sem,
    a2a_s,
    a2a_r,
    ag_s,
    ag_r,
    rs_s,
    rs_r,
    bk_s,
    bk_r,
):
    S = E * CAP
    T, D = tok_h.shape
    U = wg_h.shape[2]
    N = R * S
    me_r = lax.axis_index("rep")
    me_e = lax.axis_index("exp")
    loads = [
        pltpu.make_async_copy(tok_h, tg_v.at[0], in_sem.at[0]),
        pltpu.make_async_copy(grad_h, tg_v.at[1], in_sem.at[1]),
        pltpu.make_async_copy(wg_h.at[0], wg_v, in_sem.at[2]),
        pltpu.make_async_copy(wu_h.at[0], wu_v, in_sem.at[3]),
        pltpu.make_async_copy(wd_h.at[0], wd_v, in_sem.at[4]),
    ]
    for c in loads:
        c.start()
    barrier = pltpu.get_barrier_semaphore()
    for k in range(1, E):
        pl.semaphore_signal(
            barrier, inc=1, device_id=(me_r, lax.rem(me_e + k, E)), device_id_type=MESH
        )
    for j in range(1, R):
        pl.semaphore_signal(
            barrier, inc=1, device_id=(lax.rem(me_r + j, R), me_e), device_id_type=MESH
        )

    live = routes[...] < E
    eid = jnp.sum(jnp.where(live, routes[...].astype(F32) + 1.0, 0.0), axis=1, keepdims=True) - 1.0
    w = jnp.sum(jnp.where(live, gates[...], 0.0), axis=1, keepdims=True)
    lanes = lax.broadcasted_iota(jnp.int32, (T, T), 1)
    subs = lax.broadcasted_iota(jnp.int32, (T, T), 0)
    picked = jnp.where(eid == lanes.astype(F32), 1.0, 0.0)
    lower = jnp.where(lanes < subs, 1.0, 0.0).astype(BF16)
    before = jnp.dot(lower, picked.astype(BF16), preferred_element_type=F32)
    pos = jnp.sum(picked * before, axis=1, keepdims=True)
    slot = jnp.where(eid >= 0.0, eid * CAP + pos, -1.0)
    place_o[...] = jnp.where(slot == lanes[:, :S].astype(F32), 1.0, 0.0).astype(BF16)
    w_o[...] = w
    slot_t = jnp.transpose(jnp.broadcast_to(slot, (T, T)))[:S]
    w_t = jnp.transpose(jnp.broadcast_to(w, (T, T)))[:S]
    placed_t = slot_t == subs[:S].astype(F32)
    place_t = jnp.where(placed_t, 1.0, 0.0).astype(BF16)
    slot_gate = jnp.sum(jnp.where(placed_t, w_t, 0.0), axis=1, keepdims=True)

    pl.semaphore_wait(barrier, E + R - 2)

    def forward(t, src, p):
        for j in range(1, R):
            pltpu.make_async_remote_copy(
                src_ref=src,
                dst_ref=land.at[t, me_r, p],
                send_sem=ag_s.at[t],
                recv_sem=ag_r.at[t, j - 1],
                device_id=(lax.rem(me_r + j, R), me_e),
                device_id_type=MESH,
            ).start()

    own = []
    for t in range(2):
        loads[t].wait()
        v = jnp.dot(place_t, tg_v[t], preferred_element_type=F32)
        if t == 1:
            v = slot_gate * v
        for p in range(E):
            sendb[t, p] = v[CAP * p : CAP * p + CAP].astype(BF16)
        for k in range(1, E):
            p = lax.rem(me_e + k, E)
            pltpu.make_async_remote_copy(
                src_ref=sendb.at[t, p],
                dst_ref=land.at[t, me_r, me_e],
                send_sem=a2a_s.at[t],
                recv_sem=a2a_r.at[t, k - 1],
                device_id=(me_r, p),
                device_id_type=MESH,
            ).start()
        c = pltpu.make_async_copy(sendb.at[t, me_e], land.at[t, me_r, me_e], own_sem.at[t])
        c.start()
        own.append(c)
        forward(t, sendb.at[t, me_e], me_e)

    for t in range(2):
        for k in range(1, E):
            p = lax.rem(me_e + E - k, E)
            pltpu.make_async_copy(land.at[t, me_r, p], land.at[t, me_r, p], a2a_r.at[t, k - 1]).wait()
            forward(t, land.at[t, me_r, p], p)

    def assemble(t):
        own[t].wait()
        for j in range(R):
            r = lax.rem(me_r + R - j, R)
            if j > 0:
                pltpu.make_async_copy(land.at[t, r], land.at[t, r], ag_r.at[t, j - 1]).wait()
            for p in range(E):
                xf[CAP * p : CAP * p + CAP, :] = land[t, r, p].astype(F32)
            rows_o[t, r] = xf[...].astype(BF16)

    def send_parts(t):
        for j in range(1, R):
            r = lax.rem(me_r + j, R)
            pltpu.make_async_remote_copy(
                src_ref=part.at[t, r],
                dst_ref=rs.at[t, j - 1],
                send_sem=rs_s.at[t],
                recv_sem=rs_r.at[t, j - 1],
                device_id=(r, me_e),
                device_id_type=MESH,
            ).start()

    CH = 512

    assemble(0)
    loads[2].wait()
    loads[3].wait()
    x = rows_o[0].reshape(N, D)
    gate_pre = jnp.dot(x, wg_v[...], preferred_element_type=F32)
    up_pre = jnp.dot(x, wu_v[...], preferred_element_type=F32)
    sig = jax.nn.sigmoid(gate_pre)
    active = gate_pre * sig
    hidden = (active * up_pre).astype(BF16)
    hid_o[...] = hidden
    loads[4].wait()
    for c in range(D // CH):
        cols = slice(c * CH, c * CH + CH)
        o = jnp.dot(hidden, wd_v[:, cols], preferred_element_type=F32)
        part[0, :, :, cols] = o.astype(BF16).reshape(R, S, CH)
    send_parts(0)

    assemble(1)
    g = rows_o[1].reshape(N, D)
    hg = lax.dot_general(g, wd_v[...], LAST, preferred_element_type=F32)
    gg = (hg * up_pre * sig * (1.0 + gate_pre * (1.0 - sig))).astype(BF16)
    ug = (hg * active).astype(BF16)
    gg_o[...] = gg
    ug_o[...] = ug
    for c in range(D // CH):
        cols = slice(c * CH, c * CH + CH)
        o = lax.dot_general(gg, wg_v[cols, :], LAST, preferred_element_type=F32)
        o = o + lax.dot_general(ug, wu_v[cols, :], LAST, preferred_element_type=F32)
        part[1, :, :, cols] = o.astype(BF16).reshape(R, S, CH)
    send_parts(1)

    for t in range(2):
        total = part[t, me_r].astype(F32)
        for j in range(1, R):
            pltpu.make_async_copy(rs.at[t, j - 1], rs.at[t, j - 1], rs_r.at[t, j - 1]).wait()
            total = total + rs[t, j - 1].astype(F32)
        for p in range(E):
            back[t, p] = total[CAP * p : CAP * p + CAP].astype(BF16)
        for k in range(1, E):
            p = lax.rem(me_e + k, E)
            pltpu.make_async_remote_copy(
                src_ref=back.at[t, p],
                dst_ref=ret.at[t, me_e],
                send_sem=bk_s.at[t],
                recv_sem=bk_r.at[t, k - 1],
                device_id=(me_r, p),
                device_id_type=MESH,
            ).start()
        pltpu.make_async_copy(back.at[t, me_e], ret.at[t, me_e], own_sem.at[2 + t]).start()

    for t in range(2):
        pltpu.make_async_copy(back.at[t, me_e], ret.at[t, me_e], own_sem.at[2 + t]).wait()
        for k in range(1, E):
            p = lax.rem(me_e + E - k, E)
            pltpu.make_async_copy(ret.at[t, p], ret.at[t, p], bk_r.at[t, k - 1]).wait()
        for p in range(E):
            xf[CAP * p : CAP * p + CAP, :] = ret[t, p].astype(F32)
        ret_o[t] = xf[...].astype(BF16)

    for t in range(2):
        few = pl.ds(0, E - 1)
        pltpu.make_async_copy(sendb.at[t, few], sendb.at[t, few], a2a_s.at[t]).wait()
        pltpu.make_async_copy(back.at[t, few], back.at[t, few], bk_s.at[t]).wait()
        most = pl.ds(0, R - 1)
        pltpu.make_async_copy(land.at[t, most], land.at[t, most], ag_s.at[t]).wait()
        pltpu.make_async_copy(part.at[t, most], part.at[t, most], rs_s.at[t]).wait()


def write_kernel(
    rows, grads, hid, gg, ug, ret, place, w, comb_o, tgrad_o, wg_o, wu_o, wd_o
):
    x = rows[0]
    wg_o[0] = lax.dot_general(x, gg[...], FIRST, preferred_element_type=F32).astype(BF16)
    wu_o[0] = lax.dot_general(x, ug[...], FIRST, preferred_element_type=F32).astype(BF16)
    wd_o[0] = lax.dot_general(hid[...], grads[0], FIRST, preferred_element_type=F32).astype(BF16)
    comb_o[...] = (
        jnp.dot(place[...], ret[0], preferred_element_type=F32) * w[...]
    ).astype(BF16)
    tgrad_o[...] = jnp.dot(place[...], ret[1], preferred_element_type=F32).astype(BF16)


def on_device(R, E, tokens, routes, gates, gate_weight, up_weight, down_weight, grad_out):
    T, D = tokens.shape
    U = gate_weight.shape[2]
    S = E * CAP
    N = R * S
    vm = pl.BlockSpec(memory_space=pltpu.VMEM)
    hb = pl.BlockSpec(memory_space=pl.ANY)
    dma = pltpu.SemaphoreType.DMA
    sds = jax.ShapeDtypeStruct
    rows, hid, gg, ug, ret, place, w = pl.pallas_call(
        functools.partial(exchange_kernel, R, E),
        out_shape=(
            sds((2, R, S, D), BF16),
            sds((N, U), BF16),
            sds((N, U), BF16),
            sds((N, U), BF16),
            sds((2, S, D), BF16),
            sds((T, S), BF16),
            sds((T, 1), F32),
        ),
        in_specs=[vm, vm, hb, hb, hb, hb, hb],
        out_specs=[vm] * 7,
        scratch_shapes=[
            pltpu.VMEM((2, T, D), BF16),
            pltpu.VMEM((D, U), BF16),
            pltpu.VMEM((D, U), BF16),
            pltpu.VMEM((U, D), BF16),
            pltpu.VMEM((2, E, CAP, D), BF16),
            pltpu.VMEM((2, R, E, CAP, D), BF16),
            pltpu.VMEM((S, D), F32),
            pltpu.VMEM((2, R, S, D), BF16),
            pltpu.VMEM((2, R - 1, S, D), BF16),
            pltpu.VMEM((2, E, CAP, D), BF16),
            pltpu.VMEM((2, E, CAP, D), BF16),
            dma((5,)),
            dma((4,)),
            dma((2,)),
            dma((2, E - 1)),
            dma((2,)),
            dma((2, R - 1)),
            dma((2,)),
            dma((2, R - 1)),
            dma((2,)),
            dma((2, E - 1)),
        ],
        compiler_params=pltpu.CompilerParams(
            collective_id=0, has_side_effects=True, vmem_limit_bytes=60 * 1024 * 1024
        ),
        name="exchange",
    )(routes, gates, tokens, grad_out, gate_weight, up_weight, down_weight)
    rows = rows.reshape(2, N, D)
    CH = 512
    full = lambda *shape: pl.BlockSpec(shape, lambda i: (0,) * len(shape))
    return pl.pallas_call(
        write_kernel,
        grid=(D // CH,),
        out_shape=(
            sds((T, D), BF16),
            sds((T, D), BF16),
            sds((1, D, U), BF16),
            sds((1, D, U), BF16),
            sds((1, U, D), BF16),
        ),
        in_specs=[
            pl.BlockSpec((1, N, CH), lambda i: (0, 0, i)),
            pl.BlockSpec((1, N, CH), lambda i: (1, 0, i)),
            full(N, U),
            full(N, U),
            full(N, U),
            pl.BlockSpec((2, S, CH), lambda i: (0, 0, i)),
            full(T, S),
            full(T, 1),
        ],
        out_specs=(
            pl.BlockSpec((T, CH), lambda i: (0, i)),
            pl.BlockSpec((T, CH), lambda i: (0, i)),
            pl.BlockSpec((1, CH, U), lambda i: (0, i, 0)),
            pl.BlockSpec((1, CH, U), lambda i: (0, i, 0)),
            pl.BlockSpec((1, U, CH), lambda i: (0, 0, i)),
        ),
        name="weight_grads",
    )(rows, rows, hid, gg, ug, ret, place, w)


def solution(mesh):
    placed = (
        P(("rep", "exp"), None),
        P(("rep", "exp"), None),
        P(("rep", "exp"), None),
        P("exp", None, "rep"),
        P("exp", None, "rep"),
        P("exp", "rep", None),
        P(("rep", "exp"), None),
    )
    return jax.shard_map(
        functools.partial(on_device, mesh.shape["rep"], mesh.shape["exp"]),
        mesh=mesh,
        in_specs=placed,
        out_specs=(
            P(("rep", "exp"), None),
            P(("rep", "exp"), None),
            P("exp", None, "rep"),
            P("exp", None, "rep"),
            P("exp", "rep", None),
        ),
        check_vma=False,
    )
```

```python
import functools

import jax
import jax.numpy as jnp
from jax import lax
from jax.experimental import pallas as pl
from jax.experimental.pallas import tpu as pltpu
from jax.sharding import PartitionSpec as P

CAP = 2
MESH = pl.DeviceIdType.MESH
F32 = jnp.float32
BF16 = jnp.bfloat16
LAST = (((1,), (1,)), ((), ()))
FIRST = (((0,), (0,)), ((), ()))


def exchange_kernel(
    R,
    E,
    routes,
    gates,
    tok_h,
    grad_h,
    wg_h,
    wu_h,
    wd_h,
    rows_o,
    hid_o,
    gg_o,
    ug_o,
    ret_o,
    place_o,
    w_o,
    tg_v,
    wg_v,
    wu_v,
    wd_v,
    sendb,
    land,
    xf,
    part,
    rs,
    back,
    ret,
    in_sem,
    own_sem,
    a2a_s,
    a2a_r,
    ag_s,
    ag_r,
    rs_s,
    rs_r,
    bk_s,
    bk_r,
):
    S = E * CAP
    T, D = tok_h.shape
    U = wg_h.shape[2]
    N = R * S
    me_r = lax.axis_index("rep")
    me_e = lax.axis_index("exp")
    loads = [
        pltpu.make_async_copy(tok_h, tg_v.at[0], in_sem.at[0]),
        pltpu.make_async_copy(grad_h, tg_v.at[1], in_sem.at[1]),
        pltpu.make_async_copy(wg_h.at[0], wg_v, in_sem.at[2]),
        pltpu.make_async_copy(wu_h.at[0], wu_v, in_sem.at[3]),
        pltpu.make_async_copy(wd_h.at[0], wd_v, in_sem.at[4]),
    ]
    loads[0].start()
    loads[1].start()
    barrier = pltpu.get_barrier_semaphore()
    for k in range(1, E):
        pl.semaphore_signal(
            barrier, inc=1, device_id=(me_r, lax.rem(me_e + k, E)), device_id_type=MESH
        )
    for j in range(1, R):
        pl.semaphore_signal(
            barrier, inc=1, device_id=(lax.rem(me_r + j, R), me_e), device_id_type=MESH
        )

    live = routes[...] < E
    eid = jnp.sum(jnp.where(live, routes[...].astype(F32) + 1.0, 0.0), axis=0, keepdims=True) - 1.0
    w = jnp.sum(jnp.where(live, gates[...], 0.0), axis=0, keepdims=True)
    lanes = lax.broadcasted_iota(jnp.int32, (T, T), 1)
    subs = lax.broadcasted_iota(jnp.int32, (T, T), 0)
    picked = jnp.where(eid == subs[:S].astype(F32), 1.0, 0.0)
    upper = jnp.where(subs < lanes, 1.0, 0.0).astype(BF16)
    before = jnp.dot(picked.astype(BF16), upper, preferred_element_type=F32)
    pos = jnp.sum(picked * before, axis=0, keepdims=True)
    slot = jnp.where(eid >= 0.0, eid * CAP + pos, -1.0)
    placed_t = slot == subs[:S].astype(F32)
    place_t = jnp.where(placed_t, 1.0, 0.0).astype(BF16)
    slot_gate = jnp.sum(jnp.where(placed_t, w, 0.0), axis=1, keepdims=True)
    place_o[...] = place_t
    w_o[...] = jnp.transpose(jnp.broadcast_to(w, (T, T)))[:, :1]

    pl.semaphore_wait(barrier, E + R - 2)

    def forward(t, src, p):
        for j in range(1, R):
            pltpu.make_async_remote_copy(
                src_ref=src,
                dst_ref=land.at[t, me_r, p],
                send_sem=ag_s.at[t],
                recv_sem=ag_r.at[t, j - 1],
                device_id=(lax.rem(me_r + j, R), me_e),
                device_id_type=MESH,
            ).start()

    own = []
    for t in range(2):
        loads[t].wait()
        v = jnp.dot(place_t, tg_v[t], preferred_element_type=F32)
        if t == 1:
            v = slot_gate * v
        for p in range(E):
            sendb[t, p] = v[CAP * p : CAP * p + CAP].astype(BF16)
        for k in range(1, E):
            p = lax.rem(me_e + k, E)
            pltpu.make_async_remote_copy(
                src_ref=sendb.at[t, p],
                dst_ref=land.at[t, me_r, me_e],
                send_sem=a2a_s.at[t],
                recv_sem=a2a_r.at[t, k - 1],
                device_id=(me_r, p),
                device_id_type=MESH,
            ).start()
        c = pltpu.make_async_copy(sendb.at[t, me_e], land.at[t, me_r, me_e], own_sem.at[t])
        c.start()
        own.append(c)
        forward(t, sendb.at[t, me_e], me_e)

    for c in loads[2:]:
        c.start()
    for t in range(2):
        for k in range(1, E):
            p = lax.rem(me_e + E - k, E)
            pltpu.make_async_copy(land.at[t, me_r, p], land.at[t, me_r, p], a2a_r.at[t, k - 1]).wait()
            forward(t, land.at[t, me_r, p], p)

    def assemble(t):
        own[t].wait()
        for j in range(R):
            r = lax.rem(me_r + R - j, R)
            if j > 0:
                pltpu.make_async_copy(land.at[t, r], land.at[t, r], ag_r.at[t, j - 1]).wait()
            for p in range(E):
                xf[CAP * p : CAP * p + CAP, :] = land[t, r, p].astype(F32)
            rows_o[t, r] = xf[...].astype(BF16)

    def send_parts(t):
        for j in range(1, R):
            r = lax.rem(me_r + j, R)
            pltpu.make_async_remote_copy(
                src_ref=part.at[t, r],
                dst_ref=rs.at[t, j - 1],
                send_sem=rs_s.at[t],
                recv_sem=rs_r.at[t, j - 1],
                device_id=(r, me_e),
                device_id_type=MESH,
            ).start()

    CH = 512

    assemble(0)
    loads[2].wait()
    loads[3].wait()
    x = rows_o[0].reshape(N, D)
    gate_pre = jnp.dot(x, wg_v[...], preferred_element_type=F32)
    up_pre = jnp.dot(x, wu_v[...], preferred_element_type=F32)
    sig = jax.nn.sigmoid(gate_pre)
    active = gate_pre * sig
    hidden = (active * up_pre).astype(BF16)
    hid_o[...] = hidden
    loads[4].wait()
    for c in range(D // CH):
        cols = slice(c * CH, c * CH + CH)
        o = jnp.dot(hidden, wd_v[:, cols], preferred_element_type=F32)
        part[0, :, :, cols] = o.astype(BF16).reshape(R, S, CH)
    send_parts(0)

    assemble(1)
    g = rows_o[1].reshape(N, D)
    hg = lax.dot_general(g, wd_v[...], LAST, preferred_element_type=F32)
    gg = (hg * up_pre * sig * (1.0 + gate_pre * (1.0 - sig))).astype(BF16)
    ug = (hg * active).astype(BF16)
    gg_o[...] = gg
    ug_o[...] = ug
    for c in range(D // CH):
        cols = slice(c * CH, c * CH + CH)
        o = lax.dot_general(gg, wg_v[cols, :], LAST, preferred_element_type=F32)
        o = o + lax.dot_general(ug, wu_v[cols, :], LAST, preferred_element_type=F32)
        part[1, :, :, cols] = o.astype(BF16).reshape(R, S, CH)
    send_parts(1)

    for t in range(2):
        total = part[t, me_r].astype(F32)
        for j in range(1, R):
            pltpu.make_async_copy(rs.at[t, j - 1], rs.at[t, j - 1], rs_r.at[t, j - 1]).wait()
            total = total + rs[t, j - 1].astype(F32)
        for p in range(E):
            back[t, p] = total[CAP * p : CAP * p + CAP].astype(BF16)
        for k in range(1, E):
            p = lax.rem(me_e + k, E)
            pltpu.make_async_remote_copy(
                src_ref=back.at[t, p],
                dst_ref=ret.at[t, me_e],
                send_sem=bk_s.at[t],
                recv_sem=bk_r.at[t, k - 1],
                device_id=(me_r, p),
                device_id_type=MESH,
            ).start()
        pltpu.make_async_copy(back.at[t, me_e], ret.at[t, me_e], own_sem.at[2 + t]).start()

    for t in range(2):
        pltpu.make_async_copy(back.at[t, me_e], ret.at[t, me_e], own_sem.at[2 + t]).wait()
        for k in range(1, E):
            p = lax.rem(me_e + E - k, E)
            pltpu.make_async_copy(ret.at[t, p], ret.at[t, p], bk_r.at[t, k - 1]).wait()
        for p in range(E):
            xf[CAP * p : CAP * p + CAP, :] = ret[t, p].astype(F32)
        ret_o[t] = xf[...].astype(BF16)

    for t in range(2):
        few = pl.ds(0, E - 1)
        pltpu.make_async_copy(sendb.at[t, few], sendb.at[t, few], a2a_s.at[t]).wait()
        pltpu.make_async_copy(back.at[t, few], back.at[t, few], bk_s.at[t]).wait()
        most = pl.ds(0, R - 1)
        pltpu.make_async_copy(land.at[t, most], land.at[t, most], ag_s.at[t]).wait()
        pltpu.make_async_copy(part.at[t, most], part.at[t, most], rs_s.at[t]).wait()


def write_kernel(
    rows, grads, hid, gg, ug, ret, place, w, comb_o, tgrad_o, wg_o, wu_o, wd_o
):
    x = rows[0]
    wg_o[0] = lax.dot_general(x, gg[...], FIRST, preferred_element_type=F32).astype(BF16)
    wu_o[0] = lax.dot_general(x, ug[...], FIRST, preferred_element_type=F32).astype(BF16)
    wd_o[0] = lax.dot_general(hid[...], grads[0], FIRST, preferred_element_type=F32).astype(BF16)
    comb_o[...] = (
        lax.dot_general(place[...], ret[0], FIRST, preferred_element_type=F32) * w[...]
    ).astype(BF16)
    tgrad_o[...] = lax.dot_general(place[...], ret[1], FIRST, preferred_element_type=F32).astype(BF16)


def on_device(R, E, tokens, routes, gates, gate_weight, up_weight, down_weight, grad_out):
    T, D = tokens.shape
    U = gate_weight.shape[2]
    S = E * CAP
    N = R * S
    vm = pl.BlockSpec(memory_space=pltpu.VMEM)
    hb = pl.BlockSpec(memory_space=pl.ANY)
    dma = pltpu.SemaphoreType.DMA
    sds = jax.ShapeDtypeStruct
    rows, hid, gg, ug, ret, place, w = pl.pallas_call(
        functools.partial(exchange_kernel, R, E),
        out_shape=(
            sds((2, R, S, D), BF16),
            sds((N, U), BF16),
            sds((N, U), BF16),
            sds((N, U), BF16),
            sds((2, S, D), BF16),
            sds((S, T), BF16),
            sds((T, 1), F32),
        ),
        in_specs=[vm, vm, hb, hb, hb, hb, hb],
        out_specs=[vm] * 7,
        scratch_shapes=[
            pltpu.VMEM((2, T, D), BF16),
            pltpu.VMEM((D, U), BF16),
            pltpu.VMEM((D, U), BF16),
            pltpu.VMEM((U, D), BF16),
            pltpu.VMEM((2, E, CAP, D), BF16),
            pltpu.VMEM((2, R, E, CAP, D), BF16),
            pltpu.VMEM((S, D), F32),
            pltpu.VMEM((2, R, S, D), BF16),
            pltpu.VMEM((2, R - 1, S, D), BF16),
            pltpu.VMEM((2, E, CAP, D), BF16),
            pltpu.VMEM((2, E, CAP, D), BF16),
            dma((5,)),
            dma((4,)),
            dma((2,)),
            dma((2, E - 1)),
            dma((2,)),
            dma((2, R - 1)),
            dma((2,)),
            dma((2, R - 1)),
            dma((2,)),
            dma((2, E - 1)),
        ],
        compiler_params=pltpu.CompilerParams(
            collective_id=0, has_side_effects=True, vmem_limit_bytes=60 * 1024 * 1024
        ),
        name="exchange",
    )(routes.T, gates.T, tokens, grad_out, gate_weight, up_weight, down_weight)
    rows = rows.reshape(2, N, D)
    CH = D // 4
    full = lambda *shape: pl.BlockSpec(shape, lambda i: (0,) * len(shape))
    return pl.pallas_call(
        write_kernel,
        grid=(D // CH,),
        out_shape=(
            sds((T, D), BF16),
            sds((T, D), BF16),
            sds((1, D, U), BF16),
            sds((1, D, U), BF16),
            sds((1, U, D), BF16),
        ),
        in_specs=[
            pl.BlockSpec((1, N, CH), lambda i: (0, 0, i)),
            pl.BlockSpec((1, N, CH), lambda i: (1, 0, i)),
            full(N, U),
            full(N, U),
            full(N, U),
            pl.BlockSpec((2, S, CH), lambda i: (0, 0, i)),
            full(S, T),
            full(T, 1),
        ],
        out_specs=(
            pl.BlockSpec((T, CH), lambda i: (0, i)),
            pl.BlockSpec((T, CH), lambda i: (0, i)),
            pl.BlockSpec((1, CH, U), lambda i: (0, i, 0)),
            pl.BlockSpec((1, CH, U), lambda i: (0, i, 0)),
            pl.BlockSpec((1, U, CH), lambda i: (0, 0, i)),
        ),
        name="weight_grads",
    )(rows, rows, hid, gg, ug, ret, place, w)


def solution(mesh):
    placed = (
        P(("rep", "exp"), None),
        P(("rep", "exp"), None),
        P(("rep", "exp"), None),
        P("exp", None, "rep"),
        P("exp", None, "rep"),
        P("exp", "rep", None),
        P(("rep", "exp"), None),
    )
    return jax.shard_map(
        functools.partial(on_device, mesh.shape["rep"], mesh.shape["exp"]),
        mesh=mesh,
        in_specs=placed,
        out_specs=(
            P(("rep", "exp"), None),
            P(("rep", "exp"), None),
            P("exp", None, "rep"),
            P("exp", None, "rep"),
            P("exp", "rep", None),
        ),
        check_vma=False,
    )
```
